256 devices in a mesh: src: 32 (over x, z_lo, core), snk: 4 (over y), mom: 2 (over z_hi).
Axes of the slice: x: 4, y: 4, z: 8 (z_hi: 2, z_lo: 4; z = z_hi * 4 + z_lo), core: 2. Of those that a mesh axis runs over, the one named last changes fastest.
Arguments:
- peramb: bfloat16 [96, 16, 256, 256], P(None, 'snk', 'src'), may hold values from -0.375 to 0.375
- elem_src: bfloat16 [96, 16, 256, 256], P('src', 'mom'), may hold values from -6 to 6
- elem_snk: bfloat16 [96, 16, 256, 256], P('src', 'mom'), may hold values from -6 to 6
- op_elem: int32 [64], replicated, may hold values from 0 to 15
- hlt_kernel: float32 [16, 128], replicated, may hold values from -1.5 to 1.5
Outputs:
- smeared: float32 [64, 16, 128], P('src', 'mom')
The draws below stay inside these ranges and needn't reach their ends.
All inputs are finite; a program needn't handle non-finite values.
Results may differ from the reference program's by a relative error of at most 0.004.
Values may be sent and summed in bfloat16 or wider, within the bound.
A program may use at most 128 MiB of HBM per device.

```python
import math
import jax
import jax.numpy as jnp
from jax import lax

NV = 256
OPS = 64
NELEM = 16
NK = 128
NT0 = 96
NTS = 16


def plant(entries, rng, least, largest):
    extent = entries.shape
    index_at = [jax.random.randint(jax.random.fold_in(rng, axis), (), 0, extent[axis]) for axis in range(len(extent))]
    entries = entries.at[tuple(index_at)].set(least)
    longest = extent.index(max(extent))
    index_at[longest] = (index_at[longest] + 1) % extent[longest]
    return entries.at[tuple(index_at)].set(largest)


def block_levels(stream_key, shape, pieces, smallest, largest):
    factor_of, own = 1.0, jax.random.fold_in(stream_key, 6)
    for axis_at, blocks in pieces:
        heights = jnp.exp(jax.random.uniform(jax.random.fold_in(own, axis_at), (blocks,), jnp.float32, smallest / len(pieces), largest / len(pieces)))
        factor_of = factor_of * jnp.repeat(heights, shape[axis_at] // blocks).reshape([-1 if axis == axis_at else 1 for axis in range(len(shape))])
    return factor_of


def bell_draw(key, shape, deviation, bound, shards=(), kind=jnp.bfloat16):
    loudness = block_levels(key, shape, shards, -0.22, 0.18) if shards else 1.0
    entries = jax.random.normal(key, shape, jnp.float32) * deviation * loudness
    return jnp.minimum(jnp.maximum(entries, -bound), bound).astype(kind)


def setup_inputs(seed: int = 0) -> dict:
    keys = jax.random.split(jax.random.key(seed), 6)
    peramb = bell_draw(keys[0], (NT0, NTS, NV, NV), NV ** -0.5, 0.375, ((1, 4), (2, 32)))
    elem_src = bell_draw(keys[1], (NT0, NELEM, NV, NV), 1.0, 6.0, ((0, 32), (1, 2)))
    elem_snk = bell_draw(keys[2], (NT0, NELEM, NV, NV), 1.0, 6.0, ((0, 32), (1, 2)))
    op_elem = plant(jax.random.randint(keys[3], (OPS,), 0, NELEM), jax.random.fold_in(keys[3], 1), 0, NELEM - 1).astype(jnp.int32)
    hlt_kernel = bell_draw(keys[4], (NTS, NK), NTS ** -0.5, 1.5, (), jnp.float32)
    return {"peramb": peramb, "elem_src": elem_src, "elem_snk": elem_snk, "op_elem": op_elem, "hlt_kernel": hlt_kernel}


def reference(peramb, elem_src, elem_snk, op_elem, hlt_kernel):
    source_count = peramb.shape[0]
    sep_count = peramb.shape[1]
    eigen_count = peramb.shape[3]
    norm_factor = 1.0 / (eigen_count * math.sqrt(source_count))
    highest = lax.Precision.HIGHEST

    def one_source(inputs):
        propagator, source_elems, start = inputs
        sink_index = ((start + jnp.arange(sep_count, dtype=jnp.int32)) % source_count).astype(jnp.int32)
        sink_elems = jnp.take(elem_snk, sink_index, axis=0).astype(jnp.float32)
        prop_float = propagator.astype(jnp.float32)
        half_product = jnp.einsum('sab,fbc->sfac', prop_float, source_elems.astype(jnp.float32), precision=highest).astype(jnp.bfloat16)
        sandwich = jnp.einsum('sfac,sdc->sfad', half_product.astype(jnp.float32), prop_float, precision=highest).astype(jnp.bfloat16)
        return jnp.einsum('seab,sfab->sef', sink_elems, sandwich.astype(jnp.float32), precision=highest)
    traces = lax.map(one_source, (peramb, elem_src, jnp.arange(source_count, dtype=jnp.int32)))
    picked = traces[:, :, op_elem, :]
    correlator = jnp.transpose(lax.optimization_barrier(jnp.sum(picked, axis=0)), (1, 0, 2)) * norm_factor
    return jnp.einsum('otf,tk->ofk', correlator, hlt_kernel, precision=highest)
```

```python
import functools
import math

import jax
import jax.numpy as jnp
from jax import lax
from jax.experimental import pallas as pl
from jax.experimental.pallas import tpu as pltpu
from jax.sharding import PartitionSpec as P

MESH = pl.DeviceIdType.MESH
SRC, SNK, MOM = 32, 4, 2
OWN = 3
BLOCKS = 6


def kernel(
    norm, per_ref, es_ref, ek_ref, op_ref, hlt_ref, out_ref,
    pbuf, ebuf, sbuf, hbuf, acc, part, red_a, red_b, red_c, full,
    local_sem, p_send, p_recv, e_send, e_recv, s_send, s_recv,
    py_send, py_recv, ey_send, ey_recv, r_send, r_recv,
):
    s, y, m = lax.axis_index("src"), lax.axis_index("snk"), lax.axis_index("mom")
    x, zl, core = s // 8, (s // 2) % 4, s % 2
    f32 = jnp.float32

    def near(other):
        apart = (other // 2) % 4 - zl
        return jnp.where(apart * apart == 9, 1 - m, m)

    def ids(src, snk, mom):
        return {"src": src, "snk": snk, "mom": mom}

    def remote(src, dst, send, recv, where):
        return pltpu.make_async_remote_copy(
            src_ref=src, dst_ref=dst, send_sem=send, recv_sem=recv,
            device_id=where, device_id_type=MESH,
        )

    up = ids(s, (y + 1) % SNK, m)
    down = ids(s, (y + 3) % SNK, m)
    partner = ids(s, y, 1 - m)
    onward = ids((s + SRC - 1) % SRC, y, jnp.where(s % 8 == 0, 1 - m, m))

    barrier = pltpu.get_barrier_semaphore()

    def greet(step, carry):
        other = (s + step) % SRC
        pl.semaphore_signal(barrier, inc=1, device_id=ids(other, y, near(other)), device_id_type=MESH)
        return carry

    lax.fori_loop(1, SRC, greet, 0)
    for step in range(4):
        other = x * 8 + step * 2 + core
        pl.semaphore_signal(
            barrier, inc=1, device_id=ids(other, y, 1 - near(other)), device_id_type=MESH
        )
    for step in range(1, SNK):
        pl.semaphore_signal(barrier, inc=1, device_id=ids(s, (y + step) % SNK, m), device_id_type=MESH)
    pl.semaphore_wait(barrier, SRC - 1 + 4 + SNK - 1)

    rows = pl.ds(pl.multiple_of(y * 64, 64), 64)

    def s_step(j):
        source = ek_ref.at[:, :, rows, :] if j == 1 else sbuf.at[j - 1]
        return remote(source, sbuf.at[j], s_send.at[j - 1], s_recv.at[j - 1], onward)

    def e_cross(t):
        return remote(
            es_ref.at[t, pl.ds(2 * y, 2)], ebuf.at[t, pl.ds(8 * m + 2 * y, 2)],
            e_send.at[t], e_recv.at[t], partner,
        )

    def p_wait(t):
        whole = pbuf.at[t, pl.ds(4 * y, 4)]
        return remote(whole, whole, p_send.at[t], p_recv.at[t], up)

    def p_sent(t):
        part_of = per_ref.at[pl.ds(0, SRC - 1)]
        return remote(part_of, part_of, p_send.at[t], p_recv.at[t], up)

    s_step(1).start()
    for t in range(OWN):
        e_cross(t).start()
    for t in range(OWN):
        pltpu.make_async_copy(
            per_ref.at[OWN * s + t],
            pbuf.at[t, pl.ds(4 * y, 4), pl.ds(pl.multiple_of(8 * s, 8), 8)],
            p_recv.at[t],
        ).start()

        def scatter(step, carry, t=t):
            other = (s + step) % SRC
            remote(
                per_ref.at[OWN * other + t],
                pbuf.at[t, pl.ds(4 * y, 4), pl.ds(pl.multiple_of(8 * s, 8), 8)],
                p_send.at[t], p_recv.at[t], ids(other, y, near(other)),
            ).start()
            return carry

        lax.fori_loop(1, SRC, scatter, 0)

    own_e = [
        pltpu.make_async_copy(es_ref.at[t], ebuf.at[t, pl.ds(8 * m, 8)], local_sem.at[t])
        for t in range(OWN)
    ]
    own_s = pltpu.make_async_copy(ek_ref.at[:, :, rows, :], sbuf.at[0], local_sem.at[OWN])
    for copy in own_e + [own_s]:
        copy.start()

    def ring(piece, send, recv, t):
        def copy(which):
            if which < 2:
                source, where = piece(y), (up, down)[which]
            else:
                whole = piece((y + (3, 1)[which - 2]) % SNK)
                count = whole.shape[0] // 2
                source, where = whole.at[pl.ds((which - 2) * count, count)], (up, down)[which - 2]
            return remote(source, source, send.at[t, which], recv.at[t, which], where)

        return copy

    def p_ring(t):
        return ring(lambda row: pbuf.at[t, pl.ds(4 * row, 4)], py_send, py_recv, t)

    def e_ring(t):
        base = 8 * (1 - m)
        return ring(lambda row: ebuf.at[t, pl.ds(base + 2 * row, 2)], ey_send, ey_recv, t)

    def spread(copies):
        copies(0).start()
        copies(1).start()

    def forward(copies):
        copies(0).wait_recv()
        copies(2).start()
        copies(1).wait_recv()
        copies(3).start()

    def s_next(j):
        s_step(j - 1).wait_recv()
        s_step(j).start()

    s_next(2)
    for t in range(OWN):
        p_wait(t).wait_recv()
        spread(p_ring(t))
        e_cross(t).wait_recv()
        spread(e_ring(t))
        s_next(3 + t)
    for t in range(OWN):
        forward(p_ring(t))
        forward(e_ring(t))
    for t in range(OWN):
        for copies in (p_ring(t), e_ring(t)):
            copies(2).wait_recv()
            copies(3).wait_recv()
    s_step(5).wait_recv()
    for copy in own_e + [own_s]:
        copy.wait()

    acc[...] = jnp.zeros_like(acc)
    for t in range(OWN):

        def half(f, carry, t=t):
            mine = pbuf[t, :, rows, :].reshape(16 * 64, 256)
            hbuf[f] = jnp.dot(
                mine, ebuf[t, f], preferred_element_type=f32
            ).astype(jnp.bfloat16).reshape(16, 64, 256)
            return carry

        lax.fori_loop(0, 16, half, 0)

        def pair(ts, carry, t=t):
            at = t + ts
            block = at // OWN
            slot = jnp.where(s % 8 + block >= 8, 1 - m, m)
            sink = sbuf[block, at % OWN].reshape(8 * 64, 256)
            g = jnp.dot(sink, pbuf[t, ts], preferred_element_type=f32).astype(jnp.bfloat16)
            g = g.reshape(8, 64, 256)
            total = acc[slot, ts]
            for a in range(4):
                total += lax.dot_general(
                    g[:, a * 16 : a * 16 + 16].reshape(128, 256),
                    hbuf[:, ts, a * 16 : a * 16 + 16].reshape(256, 256),
                    (((1,), (1,)), ((), ())),
                    preferred_element_type=f32,
                )
            acc[slot, ts] = total
            return carry

        lax.fori_loop(0, 16, pair, 0)

    row = lax.broadcasted_iota(jnp.int32, (128, 256), 0) % 16
    col = lax.broadcasted_iota(jnp.int32, (128, 256), 1) % 16
    keep = row == col

    def fold(i, carry):
        masked = jnp.where(keep, acc[i // 16, i % 16], 0.0)
        full[pl.ds(pl.multiple_of(i * 8, 8), 8)] = masked.reshape(8, 16, 256).sum(axis=1)
        return carry

    lax.fori_loop(0, 32, fold, 0)
    pick = (
        lax.broadcasted_iota(jnp.int32, (16, 256), 1) // 16
        == lax.broadcasted_iota(jnp.int32, (16, 256), 0)
    ).astype(f32)
    mine = lax.dot_general(
        pick, full[...], (((1,), (1,)), ((), ())),
        preferred_element_type=f32, precision=lax.Precision.HIGHEST,
    )

    def gather_sum(value, buffer, count, index, where, stage):
        part[stage] = value
        buffer[index] = value
        for step in range(1, count):
            remote(
                part.at[stage], buffer.at[index], r_send.at[stage], r_recv.at[stage],
                where((index + step) % count),
            ).start()
        most = buffer.at[pl.ds(0, count - 1)]
        done = remote(most, most, r_send.at[stage], r_recv.at[stage], up)
        done.wait_recv()
        done.wait_send()
        total = buffer[0]
        for i in range(1, count):
            total += buffer[i]
        return total

    mine = gather_sum(
        mine, red_a, 8, x * 2 + core,
        lambda i: ids((i // 2) * 8 + zl * 2 + i % 2, y, m), 0,
    )
    mine = gather_sum(
        mine, red_b, 8, m * 4 + zl,
        lambda i: ids(x * 8 + (i % 4) * 2 + core, y, i // 4), 1,
    )
    mine = gather_sum(mine, red_c, 4, y, lambda i: ids(s, i, m), 2)

    mine = mine * norm
    weights = jnp.broadcast_to(hlt_ref[...][None, :, None, :], (2, 16, 8, 128)).reshape(256, 128)
    at = lax.broadcasted_iota(jnp.int32, (256, 128), 0)
    elem = (at // 128) * 8 + at % 8
    for o in range(2):
        chosen = jnp.where(elem == op_ref[2 * s + o], weights, 0.0)
        full[pl.ds(0, 16), pl.ds(0, 128)] = jnp.dot(
            mine, chosen, preferred_element_type=f32, precision=lax.Precision.HIGHEST
        )
        out_ref[o] = full[pl.ds(pl.multiple_of(8 * m, 8), 8), pl.ds(0, 128)]

    for j in range(1, BLOCKS):
        s_step(j).wait_send()
    for t in range(OWN):
        e_cross(t).wait_send()
        for copies in (p_ring(t), e_ring(t)):
            for which in range(4):
                copies(which).wait_send()
        p_sent(t).wait_send()


def body(norm, peramb, elem_src, elem_snk, op_elem, hlt_kernel):
    bf16, f32 = jnp.bfloat16, jnp.float32
    dma = pltpu.SemaphoreType.DMA
    anywhere = pl.BlockSpec(memory_space=pl.ANY)
    return pl.pallas_call(
        functools.partial(kernel, norm),
        out_shape=jax.ShapeDtypeStruct((2, 8, 128), f32),
        in_specs=[
            anywhere, anywhere, anywhere,
            pl.BlockSpec(memory_space=pltpu.SMEM),
            pl.BlockSpec(memory_space=pltpu.VMEM),
        ],
        out_specs=pl.BlockSpec(memory_space=pltpu.VMEM),
        scratch_shapes=[
            pltpu.VMEM((OWN, 16, 256, 256), bf16),
            pltpu.VMEM((OWN, 16, 256, 256), bf16),
            pltpu.VMEM((BLOCKS, OWN, 8, 64, 256), bf16),
            pltpu.VMEM((16, 16, 64, 256), bf16),
            pltpu.VMEM((2, 16, 128, 256), f32),
            pltpu.VMEM((3, 16, 256), f32),
            pltpu.VMEM((8, 16, 256), f32),
            pltpu.VMEM((8, 16, 256), f32),
            pltpu.VMEM((4, 16, 256), f32),
            pltpu.VMEM((256, 256), f32),
            dma((OWN + 1,)), dma((OWN,)), dma((OWN,)), dma((OWN,)), dma((OWN,)),
            dma((BLOCKS - 1,)), dma((BLOCKS - 1,)),
            dma((OWN, 4)), dma((OWN, 4)), dma((OWN, 4)), dma((OWN, 4)),
            dma((3,)), dma((3,)),
        ],
        compiler_params=pltpu.CompilerParams(
            collective_id=0, has_side_effects=True, vmem_limit_bytes=56 * 1024 * 1024
        ),
    )(peramb, elem_src, elem_snk, op_elem, hlt_kernel)


def solution(mesh):
    placed = (
        P(None, "snk", "src", None),
        P("src", "mom", None, None),
        P("src", "mom", None, None),
        P(),
        P(),
    )
    norm = 1.0 / (256 * math.sqrt(96))
    return jax.shard_map(
        functools.partial(body, norm), mesh=mesh, in_specs=placed,
        out_specs=P("src", "mom", None), check_vma=False,
    )
```

```python
import functools
import math

import jax
import jax.numpy as jnp
from jax import lax
from jax.experimental import pallas as pl
from jax.experimental.pallas import tpu as pltpu
from jax.sharding import PartitionSpec as P

MESH = pl.DeviceIdType.MESH
SRC, SNK, MOM = 32, 4, 2
OWN = 3
BLOCKS = 6
BRIDGED = (0, 1)


def kernel(
    norm, per_ref, es_ref, ek_ref, op_ref, hlt_ref, out_ref,
    pbuf, ebuf, sbuf, hbuf, acc, part, red_a, red_b, red_c, full,
    local_sem, p_send, p_recv, e_send, e_recv, s_send, s_recv,
    py_send, py_recv, ey_send, ey_recv, r_send, r_recv, ebridge, b_send, b_recv,
):
    s, y, m = lax.axis_index("src"), lax.axis_index("snk"), lax.axis_index("mom")
    x, zl, core = s // 8, (s // 2) % 4, s % 2
    f32 = jnp.float32

    z = 4 * m + zl
    lean = 2 - 4 * (z % 2)

    def near(other, sign):
        apart = ((other // 2) % 4 + 4 - zl) % 4
        hops = jnp.where(apart == 2, sign * lean, jnp.where(apart == 3, -1, apart))
        return ((z + 8 + hops) % 8) // 4

    def ids(src, snk, mom):
        return {"src": src, "snk": snk, "mom": mom}

    def remote(src, dst, send, recv, where):
        return pltpu.make_async_remote_copy(
            src_ref=src, dst_ref=dst, send_sem=send, recv_sem=recv,
            device_id=where, device_id_type=MESH,
        )

    up = ids(s, (y + 1) % SNK, m)
    down = ids(s, (y + 3) % SNK, m)
    partner = ids(s, y, 1 - m)
    onward = ids((s + SRC - 1) % SRC, y, jnp.where(s % 8 == 0, 1 - m, m))

    barrier = pltpu.get_barrier_semaphore()

    def greet(step, carry):
        other = (s + step) % SRC
        pl.semaphore_signal(barrier, inc=1, device_id=ids(other, y, near(other, -1)), device_id_type=MESH)
        return carry

    lax.fori_loop(1, SRC, greet, 0)
    for step in range(4):
        other = x * 8 + step * 2 + core
        pl.semaphore_signal(
            barrier, inc=1, device_id=ids(other, y, 1 - near(other, -1)), device_id_type=MESH
        )
    for step in range(1, SNK):
        pl.semaphore_signal(barrier, inc=1, device_id=ids(s, (y + step) % SNK, m), device_id_type=MESH)
    pl.semaphore_wait(barrier, SRC - 1 + 4 + SNK - 1)

    rows = pl.ds(pl.multiple_of(y * 64, 64), 64)

    def s_step(j):
        source = ek_ref.at[:, :, rows, :] if j == 1 else sbuf.at[j - 1]
        return remote(source, sbuf.at[j], s_send.at[j - 1], s_recv.at[j - 1], onward)

    def along_z(hops):
        to = (z + hops) % 8
        return ids(x * 8 + (to % 4) * 2 + core, y, to // 4)

    def e_first(t):
        return remote(
            es_ref.at[t, pl.ds(2 * y, 2)], ebridge.at[t], b_send.at[t], b_recv.at[t], along_z(2),
        )

    def e_cross(t):
        if t not in BRIDGED:
            source, home, where = es_ref.at[t, pl.ds(2 * y, 2)], m, partner
        else:
            source, home, where = ebridge.at[t], ((z + 6) % 8) // 4, along_z(2)
        return remote(
            source, ebuf.at[t, pl.ds(8 * home + 2 * y, 2)], e_send.at[t], e_recv.at[t], where,
        )

    def p_wait(t):
        whole = pbuf.at[t, pl.ds(4 * y, 4)]
        return remote(whole, whole, p_send.at[t], p_recv.at[t], up)

    def p_sent(t):
        part_of = per_ref.at[pl.ds(0, SRC - 1)]
        return remote(part_of, part_of, p_send.at[t], p_recv.at[t], up)

    def p_scatter(t):
        where = pbuf.at[t, pl.ds(4 * y, 4), pl.ds(pl.multiple_of(8 * s, 8), 8)]
        pltpu.make_async_copy(per_ref.at[OWN * s + t], where, p_recv.at[t]).start()

        def scatter(step, carry):
            other = (s + step) % SRC
            remote(
                per_ref.at[OWN * other + t], where,
                p_send.at[t], p_recv.at[t], ids(other, y, near(other, 1)),
            ).start()
            return carry

        lax.fori_loop(1, SRC, scatter, 0)

    own_e = [
        pltpu.make_async_copy(es_ref.at[t], ebuf.at[t, pl.ds(8 * m, 8)], local_sem.at[t])
        for t in range(OWN)
    ]
    own_s = pltpu.make_async_copy(ek_ref.at[:, :, rows, :], sbuf.at[0], local_sem.at[OWN])

    def e_begin(t):
        (e_first if t in BRIDGED else e_cross)(t).start()

    def e_bridge(t):
        e_first(t).wait_recv()
        e_cross(t).start()

    def ring(piece, send, recv, t):
        def copy(which):
            if which < 2:
                source, where = piece(y), (up, down)[which]
            else:
                whole = piece((y + (3, 1)[which - 2]) % SNK)
                count = whole.shape[0] // 2
                source, where = whole.at[pl.ds((which - 2) * count, count)], (up, down)[which - 2]
            return remote(source, source, send.at[t, which], recv.at[t, which], where)

        return copy

    def p_ring(t):
        return ring(lambda row: pbuf.at[t, pl.ds(4 * row, 4)], py_send, py_recv, t)

    def e_ring(t):
        base = 8 * (1 - m)
        return ring(lambda row: ebuf.at[t, pl.ds(base + 2 * row, 2)], ey_send, ey_recv, t)

    def spread(copies):
        copies(0).start()
        copies(1).start()

    def forward(copies):
        copies(0).wait_recv()
        copies(2).start()
        copies(1).wait_recv()
        copies(3).start()

    def s_next(j):
        s_step(j - 1).wait_recv()
        s_step(j).start()

    def p_spread(t):
        p_wait(t).wait_recv()
        spread(p_ring(t))

    def e_spread(t):
        e_cross(t).wait_recv()
        spread(e_ring(t))

    def p_forward(t):
        forward(p_ring(t))

    def e_forward(t):
        forward(e_ring(t))

    def finish(copies):
        copies(2).wait_recv()
        copies(3).wait_recv()

    def halves(t, first):
        mine = pbuf[t, :, rows, :].reshape(16 * 64, 256)

        def half(i, carry):
            f = first + i
            hbuf[t, f] = jnp.dot(
                mine, ebuf[t, f], preferred_element_type=f32
            ).astype(jnp.bfloat16).reshape(16, 64, 256)
            return carry

        lax.fori_loop(0, 8, half, 0, unroll=2)

    def pairs(t, begin, end):
        def pair(ts, carry):
            at = t + ts
            block = at // OWN
            slot = jnp.where(s % 8 + block >= 8, 1 - m, m)
            sink = sbuf[block, at % OWN].reshape(8 * 64, 256)
            g = jnp.dot(sink, pbuf[t, ts], preferred_element_type=f32).astype(jnp.bfloat16)
            g = g.reshape(8, 64, 256)
            total = acc[slot, ts]
            for a in range(4):
                total += lax.dot_general(
                    g[:, a * 16 : a * 16 + 16].reshape(128, 256),
                    hbuf[t, :, ts, a * 16 : a * 16 + 16].reshape(256, 256),
                    (((1,), (1,)), ((), ())),
                    preferred_element_type=f32,
                )
            acc[slot, ts] = total
            return carry

        lax.fori_loop(begin, end, pair, 0, unroll=2)

    p_scatter(0)
    s_step(1).start()
    p_scatter(1)
    e_begin(0)
    p_scatter(2)
    e_begin(1)
    e_begin(2)
    own_s.start()
    own_e[0].start()
    own_e[1].start()
    own_e[2].start()
    acc[...] = jnp.zeros_like(acc)
    p_spread(0)
    s_next(2)
    p_spread(1)
    e_bridge(0)
    p_forward(0)
    p_spread(2)
    e_bridge(1)
    s_next(3)
    e_spread(0)
    p_forward(1)
    e_spread(2)
    e_forward(0)
    s_next(4)
    own_s.wait()
    own_e[0].wait()
    own_e[1].wait()
    own_e[2].wait()
    finish(p_ring(0))
    halves(0, 8 * m)
    p_forward(2)
    e_spread(1)
    e_forward(2)
    finish(p_ring(1))
    halves(1, 8 * m)
    s_next(5)
    e_forward(1)
    finish(e_ring(0))
    halves(0, 8 - 8 * m)
    pairs(0, 0, 8)
    finish(e_ring(2))
    finish(p_ring(2))
    halves(2, 8 * m)
    halves(2, 8 - 8 * m)
    pairs(0, 8, 14)
    pairs(2, 0, 12)
    finish(e_ring(1))
    halves(1, 8 - 8 * m)
    pairs(1, 0, 14)
    s_step(5).wait_recv()
    pairs(0, 14, 16)
    pairs(1, 14, 16)
    pairs(2, 12, 16)

    row = lax.broadcasted_iota(jnp.int32, (128, 256), 0) % 16
    col = lax.broadcasted_iota(jnp.int32, (128, 256), 1) % 16
    keep = row == col

    def fold(i, carry):
        masked = jnp.where(keep, acc[i // 16, i % 16], 0.0)
        full[pl.ds(pl.multiple_of(i * 8, 8), 8)] = masked.reshape(8, 16, 256).sum(axis=1)
        return carry

    lax.fori_loop(0, 32, fold, 0)
    pick = (
        lax.broadcasted_iota(jnp.int32, (16, 256), 1) // 16
        == lax.broadcasted_iota(jnp.int32, (16, 256), 0)
    ).astype(f32)
    mine = lax.dot_general(
        pick, full[...], (((1,), (1,)), ((), ())),
        preferred_element_type=f32, precision=lax.Precision.HIGHEST,
    )

    def gather_sum(value, buffer, count, index, where, stage):
        part[stage] = value
        buffer[index] = value
        for step in range(1, count):
            remote(
                part.at[stage], buffer.at[index], r_send.at[stage], r_recv.at[stage],
                where((index + step) % count),
            ).start()
        most = buffer.at[pl.ds(0, count - 1)]
        done = remote(most, most, r_send.at[stage], r_recv.at[stage], up)
        done.wait_recv()
        done.wait_send()
        total = buffer[0]
        for i in range(1, count):
            total += buffer[i]
        return total

    mine = gather_sum(
        mine, red_a, 8, x * 2 + core,
        lambda i: ids((i // 2) * 8 + zl * 2 + i % 2, y, m), 0,
    )
    mine = gather_sum(
        mine, red_b, 8, m * 4 + zl,
        lambda i: ids(x * 8 + (i % 4) * 2 + core, y, i // 4), 1,
    )
    mine = gather_sum(mine, red_c, 4, y, lambda i: ids(s, i, m), 2)

    mine = mine * norm
    weights = jnp.broadcast_to(hlt_ref[...][None, :, None, :], (2, 16, 8, 128)).reshape(256, 128)
    at = lax.broadcasted_iota(jnp.int32, (256, 128), 0)
    elem = (at // 128) * 8 + at % 8
    for o in range(2):
        chosen = jnp.where(elem == op_ref[2 * s + o], weights, 0.0)
        full[pl.ds(0, 16), pl.ds(0, 128)] = jnp.dot(
            mine, chosen, preferred_element_type=f32, precision=lax.Precision.HIGHEST
        )
        out_ref[o] = full[pl.ds(pl.multiple_of(8 * m, 8), 8), pl.ds(0, 128)]

    for j in range(1, BLOCKS):
        s_step(j).wait_send()
    for t in range(OWN):
        e_cross(t).wait_send()
        if t in BRIDGED:
            e_first(t).wait_send()
        for copies in (p_ring(t), e_ring(t)):
            for which in range(4):
                copies(which).wait_send()
        p_sent(t).wait_send()


def body(norm, peramb, elem_src, elem_snk, op_elem, hlt_kernel):
    bf16, f32 = jnp.bfloat16, jnp.float32
    dma = pltpu.SemaphoreType.DMA
    anywhere = pl.BlockSpec(memory_space=pl.ANY)
    return pl.pallas_call(
        functools.partial(kernel, norm),
        out_shape=jax.ShapeDtypeStruct((2, 8, 128), f32),
        in_specs=[
            anywhere, anywhere, anywhere,
            pl.BlockSpec(memory_space=pltpu.SMEM),
            pl.BlockSpec(memory_space=pltpu.VMEM),
        ],
        out_specs=pl.BlockSpec(memory_space=pltpu.VMEM),
        scratch_shapes=[
            pltpu.VMEM((OWN, 16, 256, 256), bf16),
            pltpu.VMEM((OWN, 16, 256, 256), bf16),
            pltpu.VMEM((BLOCKS, OWN, 8, 64, 256), bf16),
            pltpu.VMEM((OWN, 16, 16, 64, 256), bf16),
            pltpu.VMEM((2, 16, 128, 256), f32),
            pltpu.VMEM((3, 16, 256), f32),
            pltpu.VMEM((8, 16, 256), f32),
            pltpu.VMEM((8, 16, 256), f32),
            pltpu.VMEM((4, 16, 256), f32),
            pltpu.VMEM((256, 256), f32),
            dma((OWN + 1,)), dma((OWN,)), dma((OWN,)), dma((OWN,)), dma((OWN,)),
            dma((BLOCKS - 1,)), dma((BLOCKS - 1,)),
            dma((OWN, 4)), dma((OWN, 4)), dma((OWN, 4)), dma((OWN, 4)),
            dma((3,)), dma((3,)),
            pltpu.VMEM((OWN, 2, 256, 256), bf16), dma((OWN,)), dma((OWN,)),
        ],
        compiler_params=pltpu.CompilerParams(
            collective_id=0, has_side_effects=True, vmem_limit_bytes=56 * 1024 * 1024
        ),
    )(peramb, elem_src, elem_snk, op_elem, hlt_kernel)


def solution(mesh):
    placed = (
        P(None, "snk", "src", None),
        P("src", "mom", None, None),
        P("src", "mom", None, None),
        P(),
        P(),
    )
    norm = 1.0 / (256 * math.sqrt(96))
    return jax.shard_map(
        functools.partial(body, norm), mesh=mesh, in_specs=placed,
        out_specs=P("src", "mom", None), check_vma=False,
    )
```

```python
import functools
import math

import jax
import jax.numpy as jnp
from jax import lax
from jax.experimental import pallas as pl
from jax.experimental.pallas import tpu as pltpu
from jax.sharding import PartitionSpec as P

MESH = pl.DeviceIdType.MESH
SRC, SNK, MOM = 32, 4, 2
OWN = 3
BLOCKS = 6


def kernel(
    norm, per_ref, es_ref, ek_ref, op_ref, hlt_ref, out_ref,
    pbuf, ebuf, sbuf, hbuf, acc, part, red_a, red_b, red_c, full,
    local_sem, p_send, p_recv, e_send, e_recv, s_send, s_recv,
    py_send, py_recv, ey_send, ey_recv, r_send, r_recv, gbuf, stage_a, stage_c,
):
    s, y, m = lax.axis_index("src"), lax.axis_index("snk"), lax.axis_index("mom")
    x, zl, core = s // 8, (s // 2) % 4, s % 2
    f32 = jnp.float32

    z = 4 * m + zl
    lean = 2

    def near(other, sign):
        apart = ((other // 2) % 4 + 4 - zl) % 4
        hops = jnp.where(apart == 2, sign * lean, jnp.where(apart == 3, -1, apart))
        return ((z + 8 + hops) % 8) // 4

    def ids(src, snk, mom):
        return {"src": src, "snk": snk, "mom": mom}

    def remote(src, dst, send, recv, where):
        return pltpu.make_async_remote_copy(
            src_ref=src, dst_ref=dst, send_sem=send, recv_sem=recv,
            device_id=where, device_id_type=MESH,
        )

    up = ids(s, (y + 1) % SNK, m)
    down = ids(s, (y + 3) % SNK, m)
    partner = ids(s, y, 1 - m)
    onward = ids((s + SRC - 1) % SRC, y, jnp.where(s % 8 == 0, 1 - m, m))

    barrier = pltpu.get_barrier_semaphore()

    def greet(step, carry):
        other = (s + step) % SRC
        pl.semaphore_signal(barrier, inc=1, device_id=ids(other, y, near(other, -1)), device_id_type=MESH)
        return carry

    lax.fori_loop(1, SRC, greet, 0)
    for step in range(4):
        other = x * 8 + step * 2 + core
        pl.semaphore_signal(
            barrier, inc=1, device_id=ids(other, y, 1 - near(other, -1)), device_id_type=MESH
        )
    for step in range(1, SNK):
        pl.semaphore_signal(barrier, inc=1, device_id=ids(s, (y + step) % SNK, m), device_id_type=MESH)
    rows = pl.ds(pl.multiple_of(y * 64, 64), 64)
    own_e = [
        pltpu.make_async_copy(es_ref.at[t], ebuf.at[t, pl.ds(8 * m, 8)], local_sem.at[t])
        for t in range(OWN)
    ]
    own_s = pltpu.make_async_copy(ek_ref.at[:, :, rows, :], sbuf.at[0], local_sem.at[OWN])
    for copy in own_e + [own_s]:
        copy.start()
    acc[...] = jnp.zeros_like(acc)
    pl.semaphore_wait(barrier, SRC - 1 + 4 + SNK - 1)

    def s_step(j):
        source = ek_ref.at[:, :, rows, :] if j == 1 else sbuf.at[j - 1]
        return remote(source, sbuf.at[j], s_send.at[j - 1], s_recv.at[j - 1], onward)

    def s_last():
        above = (z + 1) % 8
        return remote(
            ek_ref.at[:, :, rows, :], sbuf.at[5], s_send.at[4], s_recv.at[4],
            ids((s + SRC - 5) % SRC, y, above // 4),
        )

    def s_early():
        @pl.when(core == 0)
        def _():
            s_last().start()

    def s_late():
        s_step(4).wait_recv()

        @pl.when(core == 1)
        def _():
            s_step(5).start()

    def e_cross(t):
        return remote(
            es_ref.at[t, pl.ds(2 * y, 2)], ebuf.at[t, pl.ds(8 * m + 2 * y, 2)],
            e_send.at[t], e_recv.at[t], partner,
        )

    def p_wait(t):
        whole = pbuf.at[t, pl.ds(4 * y, 4)]
        return remote(whole, whole, p_send.at[t], p_recv.at[t], up)

    def p_sent(t):
        part_of = per_ref.at[pl.ds(0, SRC - 1)]
        return remote(part_of, part_of, p_send.at[t], p_recv.at[t], up)

    def p_scatter(t):
        where = pbuf.at[t, pl.ds(4 * y, 4), pl.ds(pl.multiple_of(8 * s, 8), 8)]
        pltpu.make_async_copy(per_ref.at[OWN * s + t], where, p_recv.at[t]).start()

        def scatter(step, carry):
            other = (s + step) % SRC
            remote(
                per_ref.at[OWN * other + t], where,
                p_send.at[t], p_recv.at[t], ids(other, y, near(other, 1)),
            ).start()
            return carry

        lax.fori_loop(1, SRC, scatter, 0)


    def e_begin(t):
        e_cross(t).start()

    def ring(piece, send, recv, t):
        def copy(which):
            if which < 2:
                source, where = piece(y), (up, down)[which]
            else:
                whole = piece((y + (3, 1)[which - 2]) % SNK)
                count = whole.shape[0] // 2
                source, where = whole.at[pl.ds((which - 2) * count, count)], (up, down)[which - 2]
            return remote(source, source, send.at[t, which], recv.at[t, which], where)

        return copy

    def p_ring(t):
        return ring(lambda row: pbuf.at[t, pl.ds(4 * row, 4)], py_send, py_recv, t)

    def e_ring(t):
        base = 8 * (1 - m)
        return ring(lambda row: ebuf.at[t, pl.ds(base + 2 * row, 2)], ey_send, ey_recv, t)

    def spread(copies):
        copies(0).start()
        copies(1).start()

    def forward(copies):
        copies(0).wait_recv()
        copies(2).start()
        copies(1).wait_recv()
        copies(3).start()

    def s_next(j):
        s_step(j - 1).wait_recv()
        s_step(j).start()

    def p_spread(t):
        p_wait(t).wait_recv()
        spread(p_ring(t))

    def e_spread(t):
        e_cross(t).wait_recv()
        spread(e_ring(t))

    def p_forward(t):
        forward(p_ring(t))

    def e_forward(t):
        forward(e_ring(t))

    def finish(copies):
        copies(2).wait_recv()
        copies(3).wait_recv()

    def halves(t, half):
        mine = pbuf[t, :, rows, :].reshape(16 * 64, 256)

        def one(i, carry):
            hbuf[t, i] = jnp.dot(
                mine, ebuf[t, 8 * half + i], preferred_element_type=f32
            ).astype(jnp.bfloat16).reshape(16, 64, 256)
            return carry

        lax.fori_loop(0, 8, one, 0, unroll=4)

    def traces(t, half, begin, end, fresh, unroll=4):
        def pair(ts, carry):
            at = t + ts
            block = at // OWN
            wraps = (s % 8 + block) // 8
            wraps = jnp.where((block == 5) & (core == 1), 1 - wraps, wraps)
            slot = (m + wraps) % 2
            if fresh:
                sink = sbuf[block, at % OWN].reshape(8 * 64, 256)
                g = jnp.dot(sink, pbuf[t, ts], preferred_element_type=f32).astype(jnp.bfloat16)
                g = g.reshape(8, 64, 256)
                gbuf[t, ts] = g
            else:
                g = gbuf[t, ts]
            total = acc[slot, half, ts]
            for a in range(4):
                total += lax.dot_general(
                    g[:, a * 16 : a * 16 + 16].reshape(128, 256),
                    hbuf[t, :, ts, a * 16 : a * 16 + 16].reshape(128, 256),
                    (((1,), (1,)), ((), ())),
                    preferred_element_type=f32,
                )
            acc[slot, half, ts] = total
            return carry

        lax.fori_loop(begin, end, pair, 0, unroll=min(unroll, end - begin))

    def own_traces(t, begin, end):
        traces(t, m, begin, end, True)

    def other_traces(t):
        halves(t, 1 - m)
        traces(t, 1 - m, 0, 16, False)

    p_scatter(0)
    p_scatter(1)
    p_scatter(2)
    e_begin(0)
    s_step(1).start()
    s_early()
    e_begin(1)
    e_begin(2)
    p_spread(0)
    p_spread(1)
    p_spread(2)
    own_s.wait()
    own_e[0].wait()
    own_e[1].wait()
    own_e[2].wait()
    s_next(2)
    p_forward(0)
    e_spread(0)
    s_next(3)
    p_forward(1)
    e_spread(1)
    s_next(4)
    e_forward(0)
    p_forward(2)
    s_late()
    finish(p_ring(0))
    halves(0, m)
    own_traces(0, 0, 12)
    e_spread(2)
    e_forward(1)
    finish(p_ring(1))
    halves(1, m)
    own_traces(1, 0, 12)
    e_forward(2)
    finish(p_ring(2))
    halves(2, m)
    own_traces(2, 0, 12)
    s_step(5).wait_recv()
    own_traces(0, 12, 16)
    own_traces(1, 12, 16)
    own_traces(2, 12, 16)
    finish(e_ring(0))
    other_traces(0)
    finish(e_ring(1))
    other_traces(1)
    finish(e_ring(2))
    other_traces(2)

    row = lax.broadcasted_iota(jnp.int32, (128, 128), 0) % 16
    col = lax.broadcasted_iota(jnp.int32, (128, 128), 1) % 16
    keep = row == col
    for half in range(2):

        def fold(i, carry, half=half):
            masked = jnp.where(keep, acc[i // 16, half, i % 16], 0.0)
            full[pl.ds(pl.multiple_of(i * 8, 8), 8), half * 128 : half * 128 + 128] = (
                masked.reshape(8, 16, 128).sum(axis=1)
            )
            return carry

        lax.fori_loop(0, 32, fold, 0, unroll=4)
    pick = (
        lax.broadcasted_iota(jnp.int32, (16, 256), 1) // 16
        == lax.broadcasted_iota(jnp.int32, (16, 256), 0)
    ).astype(f32)
    mine = lax.dot_general(
        pick, full[...], (((1,), (1,)), ((), ())),
        preferred_element_type=f32, precision=lax.Precision.HIGHEST,
    )

    part[...] = mine

    def gather_sum(source, held, buffer, count, index, where, stage):
        buffer[index] = held
        for step in range(1, count):
            to = (index + step) % count
            remote(
                source(to), buffer.at[index], r_send.at[stage], r_recv.at[stage], where(to),
            ).start()
        most = buffer.at[pl.ds(0, count - 1)]
        done = remote(most, most, r_send.at[stage], r_recv.at[stage], up)
        done.wait_recv()
        total = buffer[0]
        for i in range(1, count):
            total += buffer[i]
        return total

    def rows_of(half):
        return pl.ds(pl.multiple_of(8 * half, 8), 8)

    mine = gather_sum(
        lambda i: part.at[rows_of(i // 4)], part[rows_of(m)], red_b, 8, z,
        lambda i: ids(x * 8 + (i % 4) * 2 + core, y, i // 4), 0,
    )
    stage_a[...] = mine
    mine = gather_sum(
        lambda i: stage_a, mine, red_a, 8, x * 2 + core,
        lambda i: ids((i // 2) * 8 + zl * 2 + i % 2, y, m), 1,
    )
    stage_c[...] = mine
    mine = gather_sum(lambda i: stage_c, mine, red_c, 4, y, lambda i: ids(s, i, m), 2)

    mine = mine * norm
    weights = jnp.broadcast_to(hlt_ref[...][None, :, None, :], (2, 16, 8, 128)).reshape(256, 128)
    at = lax.broadcasted_iota(jnp.int32, (256, 128), 0)
    elem = (at // 128) * 8 + at % 8
    for o in range(2):
        chosen = jnp.where(elem == op_ref[2 * s + o], weights, 0.0)
        out_ref[o] = jnp.dot(
            mine, chosen, preferred_element_type=f32, precision=lax.Precision.HIGHEST
        )

    for buffer, count, stage in ((red_b, 8, 0), (red_a, 8, 1), (red_c, 4, 2)):
        most = buffer.at[pl.ds(0, count - 1)]
        remote(most, most, r_send.at[stage], r_recv.at[stage], up).wait_send()
    for j in range(1, BLOCKS):
        s_step(j).wait_send()
    for t in range(OWN):
        e_cross(t).wait_send()
        for copies in (p_ring(t), e_ring(t)):
            for which in range(4):
                copies(which).wait_send()
        p_sent(t).wait_send()


def body(norm, peramb, elem_src, elem_snk, op_elem, hlt_kernel):
    bf16, f32 = jnp.bfloat16, jnp.float32
    dma = pltpu.SemaphoreType.DMA
    anywhere = pl.BlockSpec(memory_space=pl.ANY)
    return pl.pallas_call(
        functools.partial(kernel, norm),
        out_shape=jax.ShapeDtypeStruct((2, 8, 128), f32),
        in_specs=[
            anywhere, anywhere, anywhere,
            pl.BlockSpec(memory_space=pltpu.SMEM),
            pl.BlockSpec(memory_space=pltpu.VMEM),
        ],
        out_specs=pl.BlockSpec(memory_space=pltpu.VMEM),
        scratch_shapes=[
            pltpu.VMEM((OWN, 16, 256, 256), bf16),
            pltpu.VMEM((OWN, 16, 256, 256), bf16),
            pltpu.VMEM((BLOCKS, OWN, 8, 64, 256), bf16),
            pltpu.VMEM((OWN, 8, 16, 64, 256), bf16),
            pltpu.VMEM((2, 2, 16, 128, 128), f32),
            pltpu.VMEM((16, 256), f32),
            pltpu.VMEM((8, 8, 256), f32),
            pltpu.VMEM((8, 8, 256), f32),
            pltpu.VMEM((4, 8, 256), f32),
            pltpu.VMEM((256, 256), f32),
            dma((OWN + 1,)), dma((OWN,)), dma((OWN,)), dma((OWN,)), dma((OWN,)),
            dma((BLOCKS - 1,)), dma((BLOCKS - 1,)),
            dma((OWN, 4)), dma((OWN, 4)), dma((OWN, 4)), dma((OWN, 4)),
            dma((3,)), dma((3,)),
            pltpu.VMEM((OWN, 16, 8, 64, 256), bf16),
            pltpu.VMEM((8, 256), f32), pltpu.VMEM((8, 256), f32),
        ],
        compiler_params=pltpu.CompilerParams(
            collective_id=0, has_side_effects=True, vmem_limit_bytes=56 * 1024 * 1024
        ),
    )(peramb, elem_src, elem_snk, op_elem, hlt_kernel)


def solution(mesh):
    placed = (
        P(None, "snk", "src", None),
        P("src", "mom", None, None),
        P("src", "mom", None, None),
        P(),
        P(),
    )
    norm = 1.0 / (256 * math.sqrt(96))
    return jax.shard_map(
        functools.partial(body, norm), mesh=mesh, in_specs=placed,
        out_specs=P("src", "mom", None), check_vma=False,
    )
```

```python
import functools
import math

import jax
import jax.numpy as jnp
from jax import lax
from jax.experimental import pallas as pl
from jax.experimental.pallas import tpu as pltpu
from jax.sharding import PartitionSpec as P

MESH = pl.DeviceIdType.MESH
SRC, SNK, MOM = 32, 4, 2
OWN = 3
BLOCKS = 6


def kernel(
    norm, per_ref, es_ref, ek_ref, op_ref, hlt_ref, out_ref,
    pbuf, ebuf, sbuf, hbuf, acc, part, red_a, red_b, red_c, full,
    local_sem, p_send, p_recv, e_send, e_recv, s_send, s_recv,
    py_send, py_recv, ey_send, ey_recv, r_send, r_recv, gbuf, stage_a, stage_c,
):
    s, y, m = lax.axis_index("src"), lax.axis_index("snk"), lax.axis_index("mom")
    x, zl, core = s // 8, (s // 2) % 4, s % 2
    f32 = jnp.float32

    z = 4 * m + zl
    lean = 2

    def near(other, sign):
        apart = ((other // 2) % 4 + 4 - zl) % 4
        hops = jnp.where(apart == 2, sign * lean, jnp.where(apart == 3, -1, apart))
        return ((z + 8 + hops) % 8) // 4

    def ids(src, snk, mom):
        return {"src": src, "snk": snk, "mom": mom}

    def remote(src, dst, send, recv, where):
        return pltpu.make_async_remote_copy(
            src_ref=src, dst_ref=dst, send_sem=send, recv_sem=recv,
            device_id=where, device_id_type=MESH,
        )

    up = ids(s, (y + 1) % SNK, m)
    down = ids(s, (y + 3) % SNK, m)
    partner = ids(s, y, 1 - m)
    onward = ids((s + SRC - 1) % SRC, y, jnp.where(s % 8 == 0, 1 - m, m))

    barrier = pltpu.get_barrier_semaphore()

    def greet(step, carry):
        other = (s + step) % SRC
        pl.semaphore_signal(barrier, inc=1, device_id=ids(other, y, near(other, -1)), device_id_type=MESH)
        return carry

    lax.fori_loop(1, SRC, greet, 0)
    for step in range(4):
        other = x * 8 + step * 2 + core
        pl.semaphore_signal(
            barrier, inc=1, device_id=ids(other, y, 1 - near(other, -1)), device_id_type=MESH
        )
    for step in range(1, SNK):
        pl.semaphore_signal(barrier, inc=1, device_id=ids(s, (y + step) % SNK, m), device_id_type=MESH)
    rows = pl.ds(pl.multiple_of(y * 64, 64), 64)
    own_e = [
        pltpu.make_async_copy(es_ref.at[t], ebuf.at[t, pl.ds(8 * m, 8)], local_sem.at[t])
        for t in range(OWN)
    ]
    own_s = pltpu.make_async_copy(ek_ref.at[:, :, rows, :], sbuf.at[0], local_sem.at[OWN])
    for copy in own_e + [own_s]:
        copy.start()
    acc[...] = jnp.zeros_like(acc)
    pl.semaphore_wait(barrier, SRC - 1 + 4 + SNK - 1)

    def s_step(j):
        source = ek_ref.at[:, :, rows, :] if j == 1 else sbuf.at[j - 1]
        return remote(source, sbuf.at[j], s_send.at[j - 1], s_recv.at[j - 1], onward)

    def s_last():
        above = (z + 1) % 8
        return remote(
            ek_ref.at[:, :, rows, :], sbuf.at[5], s_send.at[4], s_recv.at[4],
            ids((s + SRC - 5) % SRC, y, above // 4),
        )

    def s_early():
        @pl.when(core == 0)
        def _():
            s_last().start()

    def s_late():
        s_step(4).wait_recv()

        @pl.when(core == 1)
        def _():
            s_step(5).start()

    def e_cross(t):
        return remote(
            es_ref.at[t, pl.ds(2 * y, 2)], ebuf.at[t, pl.ds(8 * m + 2 * y, 2)],
            e_send.at[t], e_recv.at[t], partner,
        )

    def p_wait(t):
        whole = pbuf.at[t, pl.ds(4 * y, 4)]
        return remote(whole, whole, p_send.at[t], p_recv.at[t], up)

    def p_sent(t):
        part_of = per_ref.at[pl.ds(0, SRC - 1)]
        return remote(part_of, part_of, p_send.at[t], p_recv.at[t], up)

    def p_scatter(t):
        where = pbuf.at[t, pl.ds(4 * y, 4), pl.ds(pl.multiple_of(8 * s, 8), 8)]
        pltpu.make_async_copy(per_ref.at[OWN * s + t], where, p_recv.at[t]).start()

        def scatter(step, carry):
            other = (s + step) % SRC
            remote(
                per_ref.at[OWN * other + t], where,
                p_send.at[t], p_recv.at[t], ids(other, y, near(other, 1)),
            ).start()
            return carry

        lax.fori_loop(1, SRC, scatter, 0)


    def e_begin(t):
        e_cross(t).start()

    def ring(piece, send, recv, t):
        def copy(which):
            back = which % 2
            row = y if which < 4 else (y + (3, 1)[back]) % SNK
            whole = piece(row)
            count = whole.shape[0] // 2
            later = which in (1, 2, 5)
            source = whole.at[pl.ds(later * count, count)]
            return remote(source, source, send.at[t, which], recv.at[t, which], (up, down)[back])

        return copy

    def p_ring(t):
        return ring(lambda row: pbuf.at[t, pl.ds(4 * row, 4)], py_send, py_recv, t)

    def e_ring(t):
        base = 8 * (1 - m)
        return ring(lambda row: ebuf.at[t, pl.ds(base + 2 * row, 2)], ey_send, ey_recv, t)

    def spread(copies):
        for which in range(4):
            copies(which).start()

    def forward(copies):
        copies(0).wait_recv()
        copies(4).start()
        copies(1).wait_recv()
        copies(5).start()

    def s_next(j):
        s_step(j - 1).wait_recv()
        s_step(j).start()

    def p_spread(t):
        p_wait(t).wait_recv()
        spread(p_ring(t))

    def e_spread(t):
        e_cross(t).wait_recv()
        spread(e_ring(t))

    def p_forward(t):
        forward(p_ring(t))

    def e_forward(t):
        forward(e_ring(t))

    def finish(copies):
        for which in range(2, 6):
            copies(which).wait_recv()

    def halves(t, half):
        mine = pbuf[t, :, rows, :].reshape(16 * 64, 256)

        def one(i, carry):
            hbuf[t, i] = jnp.dot(
                mine, ebuf[t, 8 * half + i], preferred_element_type=f32
            ).astype(jnp.bfloat16).reshape(16, 64, 256)
            return carry

        lax.fori_loop(0, 8, one, 0, unroll=4)

    def traces(t, half, begin, end, fresh, unroll=4):
        def pair(ts, carry):
            at = t + ts
            block = at // OWN
            wraps = (s % 8 + block) // 8
            wraps = jnp.where((block == 5) & (core == 1), 1 - wraps, wraps)
            slot = (m + wraps) % 2
            if fresh:
                sink = sbuf[block, at % OWN].reshape(8 * 64, 256)
                g = jnp.dot(sink, pbuf[t, ts], preferred_element_type=f32).astype(jnp.bfloat16)
                g = g.reshape(8, 64, 256)
                gbuf[t, ts] = g
            else:
                g = gbuf[t, ts]
            total = acc[slot, half, ts]
            for a in range(4):
                total += lax.dot_general(
                    g[:, a * 16 : a * 16 + 16].reshape(128, 256),
                    hbuf[t, :, ts, a * 16 : a * 16 + 16].reshape(128, 256),
                    (((1,), (1,)), ((), ())),
                    preferred_element_type=f32,
                )
            acc[slot, half, ts] = total
            return carry

        lax.fori_loop(begin, end, pair, 0, unroll=min(unroll, end - begin))

    def own_traces(t, begin, end):
        traces(t, m, begin, end, True)

    def other_traces(t):
        halves(t, 1 - m)
        traces(t, 1 - m, 0, 16, False)

    p_scatter(0)
    p_scatter(1)
    p_scatter(2)
    e_begin(0)
    s_step(1).start()
    s_early()
    e_begin(1)
    e_begin(2)
    p_spread(0)
    p_spread(1)
    p_spread(2)
    own_s.wait()
    own_e[0].wait()
    own_e[1].wait()
    own_e[2].wait()
    s_next(2)
    p_forward(0)
    p_forward(1)
    s_next(3)
    e_spread(0)
    p_forward(2)
    s_next(4)
    finish(p_ring(0))
    halves(0, m)
    e_spread(1)
    e_forward(0)
    own_traces(0, 0, 12)
    s_late()
    e_spread(2)
    finish(p_ring(1))
    halves(1, m)
    e_forward(1)
    own_traces(1, 0, 12)
    finish(p_ring(2))
    halves(2, m)
    e_forward(2)
    own_traces(2, 0, 12)
    s_step(5).wait_recv()
    own_traces(0, 12, 16)
    own_traces(1, 12, 16)
    own_traces(2, 12, 16)
    finish(e_ring(0))
    other_traces(0)
    finish(e_ring(1))
    other_traces(1)
    finish(e_ring(2))
    other_traces(2)

    row = lax.broadcasted_iota(jnp.int32, (128, 128), 0) % 16
    col = lax.broadcasted_iota(jnp.int32, (128, 128), 1) % 16
    keep = row == col
    for half in range(2):

        def fold(i, carry, half=half):
            masked = jnp.where(keep, acc[i // 16, half, i % 16], 0.0)
            full[pl.ds(pl.multiple_of(i * 8, 8), 8), half * 128 : half * 128 + 128] = (
                masked.reshape(8, 16, 128).sum(axis=1)
            )
            return carry

        lax.fori_loop(0, 32, fold, 0, unroll=4)
    pick = (
        lax.broadcasted_iota(jnp.int32, (16, 256), 1) // 16
        == lax.broadcasted_iota(jnp.int32, (16, 256), 0)
    ).astype(f32)
    mine = lax.dot_general(
        pick, full[...], (((1,), (1,)), ((), ())),
        preferred_element_type=f32, precision=lax.Precision.HIGHEST,
    )

    part[...] = mine

    def gather_sum(source, held, buffer, count, index, where, stage):
        buffer[index] = held
        for step in range(1, count):
            to = (index + step) % count
            remote(
                source(to), buffer.at[index], r_send.at[stage], r_recv.at[stage], where(to),
            ).start()
        most = buffer.at[pl.ds(0, count - 1)]
        done = remote(most, most, r_send.at[stage], r_recv.at[stage], up)
        done.wait_recv()
        total = buffer[0]
        for i in range(1, count):
            total += buffer[i]
        return total

    def rows_of(half):
        return pl.ds(pl.multiple_of(8 * half, 8), 8)

    mine = gather_sum(
        lambda i: part.at[rows_of(i // 4)], part[rows_of(m)], red_b, 8, z,
        lambda i: ids(x * 8 + (i % 4) * 2 + core, y, i // 4), 0,
    )
    stage_a[...] = mine
    mine = gather_sum(
        lambda i: stage_a, mine, red_a, 8, x * 2 + core,
        lambda i: ids((i // 2) * 8 + zl * 2 + i % 2, y, m), 1,
    )
    stage_c[...] = mine
    mine = gather_sum(lambda i: stage_c, mine, red_c, 4, y, lambda i: ids(s, i, m), 2)

    mine = mine * norm
    weights = jnp.broadcast_to(hlt_ref[...][None, :, None, :], (2, 16, 8, 128)).reshape(256, 128)
    at = lax.broadcasted_iota(jnp.int32, (256, 128), 0)
    elem = (at // 128) * 8 + at % 8
    for o in range(2):
        chosen = jnp.where(elem == op_ref[2 * s + o], weights, 0.0)
        out_ref[o] = jnp.dot(
            mine, chosen, preferred_element_type=f32, precision=lax.Precision.HIGHEST
        )

    for buffer, count, stage in ((red_b, 8, 0), (red_a, 8, 1), (red_c, 4, 2)):
        most = buffer.at[pl.ds(0, count - 1)]
        remote(most, most, r_send.at[stage], r_recv.at[stage], up).wait_send()
    for j in range(1, BLOCKS):
        s_step(j).wait_send()
    for t in range(OWN):
        e_cross(t).wait_send()
        for copies in (p_ring(t), e_ring(t)):
            for which in range(6):
                copies(which).wait_send()
        p_sent(t).wait_send()


def body(norm, peramb, elem_src, elem_snk, op_elem, hlt_kernel):
    bf16, f32 = jnp.bfloat16, jnp.float32
    dma = pltpu.SemaphoreType.DMA
    anywhere = pl.BlockSpec(memory_space=pl.ANY)
    return pl.pallas_call(
        functools.partial(kernel, norm),
        out_shape=jax.ShapeDtypeStruct((2, 8, 128), f32),
        in_specs=[
            anywhere, anywhere, anywhere,
            pl.BlockSpec(memory_space=pltpu.SMEM),
            pl.BlockSpec(memory_space=pltpu.VMEM),
        ],
        out_specs=pl.BlockSpec(memory_space=pltpu.VMEM),
        scratch_shapes=[
            pltpu.VMEM((OWN, 16, 256, 256), bf16),
            pltpu.VMEM((OWN, 16, 256, 256), bf16),
            pltpu.VMEM((BLOCKS, OWN, 8, 64, 256), bf16),
            pltpu.VMEM((OWN, 8, 16, 64, 256), bf16),
            pltpu.VMEM((2, 2, 16, 128, 128), f32),
            pltpu.VMEM((16, 256), f32),
            pltpu.VMEM((8, 8, 256), f32),
            pltpu.VMEM((8, 8, 256), f32),
            pltpu.VMEM((4, 8, 256), f32),
            pltpu.VMEM((256, 256), f32),
            dma((OWN + 1,)), dma((OWN,)), dma((OWN,)), dma((OWN,)), dma((OWN,)),
            dma((BLOCKS - 1,)), dma((BLOCKS - 1,)),
            dma((OWN, 6)), dma((OWN, 6)), dma((OWN, 6)), dma((OWN, 6)),
            dma((3,)), dma((3,)),
            pltpu.VMEM((OWN, 16, 8, 64, 256), bf16),
            pltpu.VMEM((8, 256), f32), pltpu.VMEM((8, 256), f32),
        ],
        compiler_params=pltpu.CompilerParams(
            collective_id=0, has_side_effects=True, vmem_limit_bytes=56 * 1024 * 1024
        ),
    )(peramb, elem_src, elem_snk, op_elem, hlt_kernel)


def solution(mesh):
    placed = (
        P(None, "snk", "src", None),
        P("src", "mom", None, None),
        P("src", "mom", None, None),
        P(),
        P(),
    )
    norm = 1.0 / (256 * math.sqrt(96))
    return jax.shard_map(
        functools.partial(body, norm), mesh=mesh, in_specs=placed,
        out_specs=P("src", "mom", None), check_vma=False,
    )
```

```python
import functools
import math

import jax
import jax.numpy as jnp
from jax import lax
from jax.experimental import pallas as pl
from jax.experimental.pallas import tpu as pltpu
from jax.sharding import PartitionSpec as P

MESH = pl.DeviceIdType.MESH
SRC, SNK, MOM = 32, 4, 2
OWN = 3
BLOCKS = 6


def kernel(
    norm, per_ref, es_ref, ek_ref, op_ref, hlt_ref, out_ref,
    pbuf, ebuf, sbuf, hbuf, acc, part, red_a, red_b, red_c, full,
    local_sem, p_send, p_recv, e_send, e_recv, s_send, s_recv,
    py_send, py_recv, ey_send, ey_recv, r_send, r_recv, gbuf, stage_a, stage_c,
):
    s, y, m = lax.axis_index("src"), lax.axis_index("snk"), lax.axis_index("mom")
    x, zl, core = s // 8, (s // 2) % 4, s % 2
    f32 = jnp.float32

    z = 4 * m + zl
    lean = 2

    def near(other, sign):
        apart = ((other // 2) % 4 + 4 - zl) % 4
        hops = jnp.where(apart == 2, sign * lean, jnp.where(apart == 3, -1, apart))
        return ((z + 8 + hops) % 8) // 4

    def ids(src, snk, mom):
        return {"src": src, "snk": snk, "mom": mom}

    def remote(src, dst, send, recv, where):
        return pltpu.make_async_remote_copy(
            src_ref=src, dst_ref=dst, send_sem=send, recv_sem=recv,
            device_id=where, device_id_type=MESH,
        )

    up = ids(s, (y + 1) % SNK, m)
    down = ids(s, (y + 3) % SNK, m)
    partner = ids(s, y, 1 - m)
    onward = ids((s + SRC - 1) % SRC, y, jnp.where(s % 8 == 0, 1 - m, m))

    barrier = pltpu.get_barrier_semaphore()

    def greet(step, carry):
        other = (s + step) % SRC
        pl.semaphore_signal(barrier, inc=1, device_id=ids(other, y, near(other, -1)), device_id_type=MESH)
        return carry

    lax.fori_loop(1, SRC, greet, 0)
    for step in range(4):
        other = x * 8 + step * 2 + core
        pl.semaphore_signal(
            barrier, inc=1, device_id=ids(other, y, 1 - near(other, -1)), device_id_type=MESH
        )
    for step in range(1, SNK):
        pl.semaphore_signal(barrier, inc=1, device_id=ids(s, (y + step) % SNK, m), device_id_type=MESH)
    rows = pl.ds(pl.multiple_of(y * 64, 64), 64)
    own_e = [
        pltpu.make_async_copy(es_ref.at[t], ebuf.at[t, pl.ds(8 * m, 8)], local_sem.at[t])
        for t in range(OWN)
    ]
    own_s = pltpu.make_async_copy(ek_ref.at[:, :, rows, :], sbuf.at[0], local_sem.at[OWN])
    for copy in own_e + [own_s]:
        copy.start()
    acc[...] = jnp.zeros_like(acc)
    pl.semaphore_wait(barrier, SRC - 1 + 4 + SNK - 1)

    def s_step(j):
        source = ek_ref.at[:, :, rows, :] if j == 1 else sbuf.at[j - 1]
        return remote(source, sbuf.at[j], s_send.at[j - 1], s_recv.at[j - 1], onward)

    def s_last():
        above = (z + 1) % 8
        return remote(
            ek_ref.at[:, :, rows, :], sbuf.at[5], s_send.at[4], s_recv.at[4],
            ids((s + SRC - 5) % SRC, y, above // 4),
        )

    def s_early():
        @pl.when(core == 0)
        def _():
            s_last().start()

    def s_late():
        s_step(4).wait_recv()

        @pl.when(core == 1)
        def _():
            s_step(5).start()

    def e_cross(t):
        return remote(
            es_ref.at[t, pl.ds(2 * y, 2)], ebuf.at[t, pl.ds(8 * m + 2 * y, 2)],
            e_send.at[t], e_recv.at[t], partner,
        )

    def p_wait(t):
        whole = pbuf.at[t, pl.ds(4 * y, 4)]
        return remote(whole, whole, p_send.at[t], p_recv.at[t], up)

    def p_sent(t):
        part_of = per_ref.at[pl.ds(0, SRC - 1)]
        return remote(part_of, part_of, p_send.at[t], p_recv.at[t], up)

    def p_scatter(t):
        where = pbuf.at[t, pl.ds(4 * y, 4), pl.ds(pl.multiple_of(8 * s, 8), 8)]
        pltpu.make_async_copy(per_ref.at[OWN * s + t], where, p_recv.at[t]).start()

        def scatter(step, carry):
            other = (s + step) % SRC
            remote(
                per_ref.at[OWN * other + t], where,
                p_send.at[t], p_recv.at[t], ids(other, y, near(other, 1)),
            ).start()
            return carry

        lax.fori_loop(1, SRC, scatter, 0)


    def e_begin(t):
        e_cross(t).start()

    def ring(piece, send, recv, t):
        def copy(which):
            back = which % 2
            row = y if which < 4 else (y + (3, 1)[back]) % SNK
            whole = piece(row)
            count = whole.shape[0] // 2
            later = which in (1, 2, 5)
            source = whole.at[pl.ds(later * count, count)]
            return remote(source, source, send.at[t, which], recv.at[t, which], (up, down)[back])

        return copy

    def p_ring(t):
        return ring(lambda row: pbuf.at[t, pl.ds(4 * row, 4)], py_send, py_recv, t)

    def e_ring(t):
        base = 8 * (1 - m)
        return ring(lambda row: ebuf.at[t, pl.ds(base + 2 * row, 2)], ey_send, ey_recv, t)

    def spread(copies):
        for which in range(4):
            copies(which).start()

    def forward(copies):
        copies(0).wait_recv()
        copies(4).start()
        copies(1).wait_recv()
        copies(5).start()

    def s_next(j):
        s_step(j - 1).wait_recv()
        s_step(j).start()

    def p_spread(t):
        p_wait(t).wait_recv()
        spread(p_ring(t))

    def e_spread(t):
        e_cross(t).wait_recv()
        spread(e_ring(t))

    def p_forward(t):
        forward(p_ring(t))

    def e_forward(t):
        forward(e_ring(t))

    def finish(copies):
        for which in range(2, 6):
            copies(which).wait_recv()

    def halves(t, half):
        mine = pbuf[t, :, rows, :].reshape(16 * 64, 256)

        def one(i, carry):
            hbuf[t, i] = jnp.dot(
                mine, ebuf[t, 8 * half + i], preferred_element_type=f32
            ).astype(jnp.bfloat16).reshape(16, 64, 256)
            return carry

        lax.fori_loop(0, 8, one, 0, unroll=8)

    def traces(t, half, begin, end, fresh, unroll=12):
        def pair(ts, carry):
            at = t + ts
            block = at // OWN
            wraps = (s % 8 + block) // 8
            wraps = jnp.where((block == 5) & (core == 1), 1 - wraps, wraps)
            slot = (m + wraps) % 2
            if fresh:
                sink = sbuf[block, at % OWN].reshape(8 * 64, 256)
                g = jnp.dot(sink, pbuf[t, ts], preferred_element_type=f32).astype(jnp.bfloat16)
                g = g.reshape(8, 64, 256)
                gbuf[t, ts] = g
            else:
                g = gbuf[t, ts]
            total = acc[slot, half, ts]
            for a in range(4):
                total += lax.dot_general(
                    g[:, a * 16 : a * 16 + 16].reshape(128, 256),
                    hbuf[t, :, ts, a * 16 : a * 16 + 16].reshape(128, 256),
                    (((1,), (1,)), ((), ())),
                    preferred_element_type=f32,
                )
            acc[slot, half, ts] = total
            return carry

        lax.fori_loop(begin, end, pair, 0, unroll=min(unroll, end - begin))

    def own_traces(t, begin, end):
        traces(t, m, begin, end, True)

    def other_traces(t):
        halves(t, 1 - m)
        traces(t, 1 - m, 0, 16, False, 16)

    p_scatter(0)
    p_scatter(1)
    p_scatter(2)
    e_begin(0)
    s_step(1).start()
    s_early()
    e_begin(1)
    e_begin(2)
    p_spread(0)
    p_spread(1)
    p_spread(2)
    own_s.wait()
    own_e[0].wait()
    own_e[1].wait()
    own_e[2].wait()
    s_next(2)
    p_forward(0)
    p_forward(1)
    s_next(3)
    e_spread(0)
    p_forward(2)
    s_next(4)
    finish(p_ring(0))
    halves(0, m)
    e_spread(1)
    e_forward(0)
    own_traces(0, 0, 12)
    s_late()
    e_spread(2)
    finish(p_ring(1))
    halves(1, m)
    e_forward(1)
    own_traces(1, 0, 12)
    finish(p_ring(2))
    halves(2, m)
    e_forward(2)
    own_traces(2, 0, 12)
    s_step(5).wait_recv()
    own_traces(0, 12, 16)
    own_traces(1, 12, 16)
    own_traces(2, 12, 16)
    finish(e_ring(0))
    other_traces(0)
    finish(e_ring(1))
    other_traces(1)
    finish(e_ring(2))
    other_traces(2)

    row = lax.broadcasted_iota(jnp.int32, (128, 128), 0) % 16
    col = lax.broadcasted_iota(jnp.int32, (128, 128), 1) % 16
    keep = row == col
    for half in range(2):

        def fold(i, carry, half=half):
            masked = jnp.where(keep, acc[i // 16, half, i % 16], 0.0)
            full[pl.ds(pl.multiple_of(i * 8, 8), 8), half * 128 : half * 128 + 128] = (
                masked.reshape(8, 16, 128).sum(axis=1)
            )
            return carry

        lax.fori_loop(0, 32, fold, 0, unroll=4)
    pick = (
        lax.broadcasted_iota(jnp.int32, (16, 256), 1) // 16
        == lax.broadcasted_iota(jnp.int32, (16, 256), 0)
    ).astype(f32)
    mine = lax.dot_general(
        pick, full[...], (((1,), (1,)), ((), ())),
        preferred_element_type=f32, precision=lax.Precision.HIGHEST,
    )

    part[...] = mine

    def gather_sum(source, held, buffer, count, index, where, stage):
        buffer[index] = held
        for step in range(1, count):
            to = (index + step) % count
            remote(
                source(to), buffer.at[index], r_send.at[stage], r_recv.at[stage], where(to),
            ).start()
        most = buffer.at[pl.ds(0, count - 1)]
        done = remote(most, most, r_send.at[stage], r_recv.at[stage], up)
        done.wait_recv()
        total = buffer[0]
        for i in range(1, count):
            total += buffer[i]
        return total

    def rows_of(half):
        return pl.ds(pl.multiple_of(8 * half, 8), 8)

    mine = gather_sum(
        lambda i: part.at[rows_of(i // 4)], part[rows_of(m)], red_b, 8, z,
        lambda i: ids(x * 8 + (i % 4) * 2 + core, y, i // 4), 0,
    )
    stage_a[...] = mine
    mine = gather_sum(
        lambda i: stage_a, mine, red_a, 8, x * 2 + core,
        lambda i: ids((i // 2) * 8 + zl * 2 + i % 2, y, m), 1,
    )
    stage_c[...] = mine
    mine = gather_sum(lambda i: stage_c, mine, red_c, 4, y, lambda i: ids(s, i, m), 2)

    mine = mine * norm
    weights = jnp.broadcast_to(hlt_ref[...][None, :, None, :], (2, 16, 8, 128)).reshape(256, 128)
    at = lax.broadcasted_iota(jnp.int32, (256, 128), 0)
    elem = (at // 128) * 8 + at % 8
    for o in range(2):
        chosen = jnp.where(elem == op_ref[2 * s + o], weights, 0.0)
        out_ref[o] = jnp.dot(
            mine, chosen, preferred_element_type=f32, precision=lax.Precision.HIGHEST
        )

    for buffer, count, stage in ((red_b, 8, 0), (red_a, 8, 1), (red_c, 4, 2)):
        most = buffer.at[pl.ds(0, count - 1)]
        remote(most, most, r_send.at[stage], r_recv.at[stage], up).wait_send()
    for j in range(1, BLOCKS):
        s_step(j).wait_send()
    for t in range(OWN):
        e_cross(t).wait_send()
        for copies in (p_ring(t), e_ring(t)):
            for which in range(6):
                copies(which).wait_send()
        p_sent(t).wait_send()


def body(norm, peramb, elem_src, elem_snk, op_elem, hlt_kernel):
    bf16, f32 = jnp.bfloat16, jnp.float32
    dma = pltpu.SemaphoreType.DMA
    anywhere = pl.BlockSpec(memory_space=pl.ANY)
    return pl.pallas_call(
        functools.partial(kernel, norm),
        out_shape=jax.ShapeDtypeStruct((2, 8, 128), f32),
        in_specs=[
            anywhere, anywhere, anywhere,
            pl.BlockSpec(memory_space=pltpu.SMEM),
            pl.BlockSpec(memory_space=pltpu.VMEM),
        ],
        out_specs=pl.BlockSpec(memory_space=pltpu.VMEM),
        scratch_shapes=[
            pltpu.VMEM((OWN, 16, 256, 256), bf16),
            pltpu.VMEM((OWN, 16, 256, 256), bf16),
            pltpu.VMEM((BLOCKS, OWN, 8, 64, 256), bf16),
            pltpu.VMEM((OWN, 8, 16, 64, 256), bf16),
            pltpu.VMEM((2, 2, 16, 128, 128), f32),
            pltpu.VMEM((16, 256), f32),
            pltpu.VMEM((8, 8, 256), f32),
            pltpu.VMEM((8, 8, 256), f32),
            pltpu.VMEM((4, 8, 256), f32),
            pltpu.VMEM((256, 256), f32),
            dma((OWN + 1,)), dma((OWN,)), dma((OWN,)), dma((OWN,)), dma((OWN,)),
            dma((BLOCKS - 1,)), dma((BLOCKS - 1,)),
            dma((OWN, 6)), dma((OWN, 6)), dma((OWN, 6)), dma((OWN, 6)),
            dma((3,)), dma((3,)),
            pltpu.VMEM((OWN, 16, 8, 64, 256), bf16),
            pltpu.VMEM((8, 256), f32), pltpu.VMEM((8, 256), f32),
        ],
        compiler_params=pltpu.CompilerParams(
            collective_id=0, has_side_effects=True, vmem_limit_bytes=56 * 1024 * 1024
        ),
    )(peramb, elem_src, elem_snk, op_elem, hlt_kernel)


def solution(mesh):
    placed = (
        P(None, "snk", "src", None),
        P("src", "mom", None, None),
        P("src", "mom", None, None),
        P(),
        P(),
    )
    norm = 1.0 / (256 * math.sqrt(96))
    return jax.shard_map(
        functools.partial(body, norm), mesh=mesh, in_specs=placed,
        out_specs=P("src", "mom", None), check_vma=False,
    )
```

```python
import functools
import math

import jax
import jax.numpy as jnp
from jax import lax
from jax.experimental import pallas as pl
from jax.experimental.pallas import tpu as pltpu
from jax.sharding import PartitionSpec as P

MESH = pl.DeviceIdType.MESH
SRC, SNK, MOM = 32, 4, 2
OWN = 3
BLOCKS = 6


def kernel(
    norm, per_ref, es_ref, ek_ref, op_ref, hlt_ref, out_ref,
    pbuf, ebuf, sbuf, hbuf, acc, part, red_a, red_b, red_c, full,
    local_sem, p_send, p_recv, e_send, e_recv, s_send, s_recv,
    py_send, py_recv, ey_send, ey_recv, r_send, r_recv, gbuf, stage_a, stage_c,
):
    s, y, m = lax.axis_index("src"), lax.axis_index("snk"), lax.axis_index("mom")
    x, zl, core = s // 8, (s // 2) % 4, s % 2
    f32 = jnp.float32

    z = 4 * m + zl
    lean = 2

    def near(other, sign):
        apart = ((other // 2) % 4 + 4 - zl) % 4
        hops = jnp.where(apart == 2, sign * lean, jnp.where(apart == 3, -1, apart))
        return ((z + 8 + hops) % 8) // 4

    def ids(src, snk, mom):
        return {"src": src, "snk": snk, "mom": mom}

    def remote(src, dst, send, recv, where):
        return pltpu.make_async_remote_copy(
            src_ref=src, dst_ref=dst, send_sem=send, recv_sem=recv,
            device_id=where, device_id_type=MESH,
        )

    up = ids(s, (y + 1) % SNK, m)
    down = ids(s, (y + 3) % SNK, m)
    partner = ids(s, y, 1 - m)
    onward = ids((s + SRC - 1) % SRC, y, jnp.where(s % 8 == 0, 1 - m, m))

    barrier = pltpu.get_barrier_semaphore()

    def greet(step, carry):
        other = (s + step) % SRC
        pl.semaphore_signal(barrier, inc=1, device_id=ids(other, y, near(other, -1)), device_id_type=MESH)
        return carry

    lax.fori_loop(1, SRC, greet, 0)
    for step in range(4):
        other = x * 8 + step * 2 + core
        pl.semaphore_signal(
            barrier, inc=1, device_id=ids(other, y, 1 - near(other, -1)), device_id_type=MESH
        )
    for step in range(1, SNK):
        pl.semaphore_signal(barrier, inc=1, device_id=ids(s, (y + step) % SNK, m), device_id_type=MESH)
    rows = pl.ds(pl.multiple_of(y * 64, 64), 64)
    own_e = [
        pltpu.make_async_copy(es_ref.at[t], ebuf.at[t, pl.ds(8 * m, 8)], local_sem.at[t])
        for t in range(OWN)
    ]
    own_s = pltpu.make_async_copy(ek_ref.at[:, :, rows, :], sbuf.at[0], local_sem.at[OWN])
    for copy in own_e + [own_s]:
        copy.start()
    acc[...] = jnp.zeros_like(acc)
    pl.semaphore_wait(barrier, SRC - 1 + 4 + SNK - 1)

    def s_step(j):
        source = ek_ref.at[:, :, rows, :] if j == 1 else sbuf.at[j - 1]
        return remote(source, sbuf.at[j], s_send.at[j - 1], s_recv.at[j - 1], onward)

    def s_last():
        above = (z + 1) % 8
        return remote(
            ek_ref.at[:, :, rows, :], sbuf.at[5], s_send.at[4], s_recv.at[4],
            ids((s + SRC - 5) % SRC, y, above // 4),
        )

    def s_early():
        @pl.when(core == 0)
        def _():
            s_last().start()

    def s_late():
        s_step(4).wait_recv()

        @pl.when(core == 1)
        def _():
            s_step(5).start()

    def e_cross(t):
        return remote(
            es_ref.at[t, pl.ds(2 * y, 2)], ebuf.at[t, pl.ds(8 * m + 2 * y, 2)],
            e_send.at[t], e_recv.at[t], partner,
        )

    def p_wait(t):
        whole = pbuf.at[t, pl.ds(4 * y, 4)]
        return remote(whole, whole, p_send.at[t], p_recv.at[t], up)

    def p_sent(t):
        part_of = per_ref.at[pl.ds(0, SRC - 1)]
        return remote(part_of, part_of, p_send.at[t], p_recv.at[t], up)

    def p_scatter(t):
        where = pbuf.at[t, pl.ds(4 * y, 4), pl.ds(pl.multiple_of(8 * s, 8), 8)]
        pltpu.make_async_copy(per_ref.at[OWN * s + t], where, p_recv.at[t]).start()

        def scatter(step, carry):
            other = (s + step) % SRC
            remote(
                per_ref.at[OWN * other + t], where,
                p_send.at[t], p_recv.at[t], ids(other, y, near(other, 1)),
            ).start()
            return carry

        lax.fori_loop(1, SRC, scatter, 0)


    def e_begin(t):
        e_cross(t).start()

    def ring(piece, send, recv, t):
        def copy(which):
            back = which % 2
            row = y if which < 4 else (y + (3, 1)[back]) % SNK
            whole = piece(row)
            count = whole.shape[0] // 2
            later = which in (1, 2, 5)
            source = whole.at[pl.ds(later * count, count)]
            return remote(source, source, send.at[t, which], recv.at[t, which], (up, down)[back])

        return copy

    def p_ring(t):
        return ring(lambda row: pbuf.at[t, pl.ds(4 * row, 4)], py_send, py_recv, t)

    def e_ring(t):
        base = 8 * (1 - m)
        return ring(lambda row: ebuf.at[t, pl.ds(base + 2 * row, 2)], ey_send, ey_recv, t)

    def spread(copies):
        for which in range(4):
            copies(which).start()

    def forward(copies):
        copies(0).wait_recv()
        copies(4).start()
        copies(1).wait_recv()
        copies(5).start()

    def s_next(j):
        s_step(j - 1).wait_recv()
        s_step(j).start()

    def p_spread(t):
        p_wait(t).wait_recv()
        spread(p_ring(t))

    def e_spread(t):
        e_cross(t).wait_recv()
        spread(e_ring(t))

    def p_forward(t):
        forward(p_ring(t))

    def e_forward(t):
        forward(e_ring(t))

    def finish(copies):
        for which in range(2, 6):
            copies(which).wait_recv()

    def halves(t, half):
        mine = pbuf[t, :, rows, :].reshape(16 * 64, 256)

        def one(i, carry):
            hbuf[t, i] = jnp.dot(
                mine, ebuf[t, 8 * half + i], preferred_element_type=f32
            ).astype(jnp.bfloat16).reshape(16, 64, 256)
            return carry

        lax.fori_loop(0, 8, one, 0, unroll=8)

    def traces(t, half, begin, end, fresh, unroll=16):
        def pair(ts, carry):
            at = t + ts
            block = at // OWN
            wraps = (s % 8 + block) // 8
            wraps = jnp.where((block == 5) & (core == 1), 1 - wraps, wraps)
            slot = (m + wraps) % 2
            if fresh:
                sink = sbuf[block, at % OWN].reshape(8 * 64, 256)
                g = jnp.dot(sink, pbuf[t, ts], preferred_element_type=f32).astype(jnp.bfloat16)
                g = g.reshape(8, 64, 256)
                gbuf[t, ts] = g
            else:
                g = gbuf[t, ts]
            total = acc[slot, half, ts]
            for a in range(4):
                total += lax.dot_general(
                    g[:, a * 16 : a * 16 + 16].reshape(128, 256),
                    hbuf[t, :, ts, a * 16 : a * 16 + 16].reshape(128, 256),
                    (((1,), (1,)), ((), ())),
                    preferred_element_type=f32,
                )
            acc[slot, half, ts] = total
            return carry

        lax.fori_loop(begin, end, pair, 0, unroll=min(unroll, end - begin))

    def own_traces(t, begin, end):
        traces(t, m, begin, end, True)

    def other_traces(t):
        halves(t, 1 - m)
        traces(t, 1 - m, 0, 16, False, 16)

    p_scatter(0)
    p_scatter(1)
    p_scatter(2)
    e_begin(0)
    s_step(1).start()
    s_early()
    e_begin(1)
    e_begin(2)
    p_spread(0)
    p_spread(1)
    p_spread(2)
    own_s.wait()
    own_e[0].wait()
    own_e[1].wait()
    own_e[2].wait()
    s_next(2)
    p_forward(0)
    p_forward(1)
    s_next(3)
    e_spread(0)
    p_forward(2)
    s_next(4)
    finish(p_ring(0))
    halves(0, m)
    e_spread(1)
    e_forward(0)
    own_traces(0, 0, 12)
    s_late()
    e_spread(2)
    finish(p_ring(1))
    halves(1, m)
    e_forward(1)
    own_traces(1, 0, 12)
    finish(p_ring(2))
    halves(2, m)
    e_forward(2)
    s_step(5).wait_recv()
    own_traces(2, 0, 16)
    own_traces(0, 12, 16)
    own_traces(1, 12, 16)
    finish(e_ring(0))
    other_traces(0)
    finish(e_ring(1))
    other_traces(1)
    finish(e_ring(2))
    other_traces(2)

    row = lax.broadcasted_iota(jnp.int32, (128, 128), 0) % 16
    col = lax.broadcasted_iota(jnp.int32, (128, 128), 1) % 16
    keep = row == col
    for half in range(2):

        def fold(i, carry, half=half):
            masked = jnp.where(keep, acc[i // 16, half, i % 16], 0.0)
            full[pl.ds(pl.multiple_of(i * 8, 8), 8), half * 128 : half * 128 + 128] = (
                masked.reshape(8, 16, 128).sum(axis=1)
            )
            return carry

        lax.fori_loop(0, 32, fold, 0, unroll=8)
    pick = (
        lax.broadcasted_iota(jnp.int32, (16, 256), 1) // 16
        == lax.broadcasted_iota(jnp.int32, (16, 256), 0)
    ).astype(f32)
    mine = lax.dot_general(
        pick, full[...], (((1,), (1,)), ((), ())),
        preferred_element_type=f32, precision=lax.Precision.HIGHEST,
    )

    part[...] = mine

    def gather_sum(source, held, buffer, count, index, where, stage):
        buffer[index] = held
        for step in range(1, count):
            to = (index + step) % count
            remote(
                source(to), buffer.at[index], r_send.at[stage], r_recv.at[stage], where(to),
            ).start()
        most = buffer.at[pl.ds(0, count - 1)]
        done = remote(most, most, r_send.at[stage], r_recv.at[stage], up)
        done.wait_recv()
        total = buffer[0]
        for i in range(1, count):
            total += buffer[i]
        return total

    def rows_of(half):
        return pl.ds(pl.multiple_of(8 * half, 8), 8)

    mine = gather_sum(
        lambda i: part.at[rows_of(i // 4)], part[rows_of(m)], red_b, 8, z,
        lambda i: ids(x * 8 + (i % 4) * 2 + core, y, i // 4), 0,
    )
    stage_a[...] = mine
    mine = gather_sum(
        lambda i: stage_a, mine, red_a, 8, x * 2 + core,
        lambda i: ids((i // 2) * 8 + zl * 2 + i % 2, y, m), 1,
    )
    stage_c[...] = mine
    mine = gather_sum(lambda i: stage_c, mine, red_c, 4, y, lambda i: ids(s, i, m), 2)

    mine = mine * norm
    weights = jnp.broadcast_to(hlt_ref[...][None, :, None, :], (2, 16, 8, 128)).reshape(256, 128)
    at = lax.broadcasted_iota(jnp.int32, (256, 128), 0)
    elem = (at // 128) * 8 + at % 8
    for o in range(2):
        chosen = jnp.where(elem == op_ref[2 * s + o], weights, 0.0)
        out_ref[o] = jnp.dot(
            mine, chosen, preferred_element_type=f32, precision=lax.Precision.HIGHEST
        )

    for buffer, count, stage in ((red_b, 8, 0), (red_a, 8, 1), (red_c, 4, 2)):
        most = buffer.at[pl.ds(0, count - 1)]
        remote(most, most, r_send.at[stage], r_recv.at[stage], up).wait_send()
    for j in range(1, BLOCKS):
        s_step(j).wait_send()
    for t in range(OWN):
        e_cross(t).wait_send()
        for copies in (p_ring(t), e_ring(t)):
            for which in range(6):
                copies(which).wait_send()
        p_sent(t).wait_send()


def body(norm, peramb, elem_src, elem_snk, op_elem, hlt_kernel):
    bf16, f32 = jnp.bfloat16, jnp.float32
    dma = pltpu.SemaphoreType.DMA
    anywhere = pl.BlockSpec(memory_space=pl.ANY)
    return pl.pallas_call(
        functools.partial(kernel, norm),
        out_shape=jax.ShapeDtypeStruct((2, 8, 128), f32),
        in_specs=[
            anywhere, anywhere, anywhere,
            pl.BlockSpec(memory_space=pltpu.SMEM),
            pl.BlockSpec(memory_space=pltpu.VMEM),
        ],
        out_specs=pl.BlockSpec(memory_space=pltpu.VMEM),
        scratch_shapes=[
            pltpu.VMEM((OWN, 16, 256, 256), bf16),
            pltpu.VMEM((OWN, 16, 256, 256), bf16),
            pltpu.VMEM((BLOCKS, OWN, 8, 64, 256), bf16),
            pltpu.VMEM((OWN, 8, 16, 64, 256), bf16),
            pltpu.VMEM((2, 2, 16, 128, 128), f32),
            pltpu.VMEM((16, 256), f32),
            pltpu.VMEM((8, 8, 256), f32),
            pltpu.VMEM((8, 8, 256), f32),
            pltpu.VMEM((4, 8, 256), f32),
            pltpu.VMEM((256, 256), f32),
            dma((OWN + 1,)), dma((OWN,)), dma((OWN,)), dma((OWN,)), dma((OWN,)),
            dma((BLOCKS - 1,)), dma((BLOCKS - 1,)),
            dma((OWN, 6)), dma((OWN, 6)), dma((OWN, 6)), dma((OWN, 6)),
            dma((3,)), dma((3,)),
            pltpu.VMEM((OWN, 16, 8, 64, 256), bf16),
            pltpu.VMEM((8, 256), f32), pltpu.VMEM((8, 256), f32),
        ],
        compiler_params=pltpu.CompilerParams(
            collective_id=0, has_side_effects=True, vmem_limit_bytes=56 * 1024 * 1024
        ),
    )(peramb, elem_src, elem_snk, op_elem, hlt_kernel)


def solution(mesh):
    placed = (
        P(None, "snk", "src", None),
        P("src", "mom", None, None),
        P("src", "mom", None, None),
        P(),
        P(),
    )
    norm = 1.0 / (256 * math.sqrt(96))
    return jax.shard_map(
        functools.partial(body, norm), mesh=mesh, in_specs=placed,
        out_specs=P("src", "mom", None), check_vma=False,
    )
```
